32 devices in a mesh: group: 8 (over z, y), expert: 4 (over x, core).
Axes of the slice: x: 2, y: 2, z: 4, core: 2. Of those that a mesh axis runs over, the one named last changes fastest.
Arguments:
- images: bfloat16 [6304, 768], P(('group', 'expert')), may hold values from -6 to 6
- first_gain: float32 [768], replicated, may hold values from 0.5 to 1.5
- first_shift: float32 [768], replicated, may hold values from -1.75 to 1.75
- qkv_weight: bfloat16 [768, 2304], replicated, may hold values from -0.21875 to 0.21875
- proj_weight: bfloat16 [768, 768], replicated, may hold values from -0.875 to 0.875
- proj_bias: float32 [768], replicated, may hold values from -1.75 to 1.75
- second_gain: float32 [768], replicated, may hold values from 0.5 to 1.5
- second_shift: float32 [768], replicated, may hold values from -1.75 to 1.75
- router_weight: bfloat16 [768, 4], replicated, may hold values from -0.15625 to 0.15625
- expert_up: bfloat16 [4, 768, 3072], P('expert'), may hold values from -0.21875 to 0.21875
- up_bias: float32 [4, 3072], P('expert'), may hold values from -0.625 to 0.625
- expert_down: bfloat16 [4, 3072, 768], P('expert'), may hold values from -0.875 to 0.875
- down_bias: float32 [4, 768], P('expert'), may hold values from -1.75 to 1.75
- expert_ids: int32 [6304, 2], P(('group', 'expert')), may hold values from 0 to 3, all different within a row; in each aligned block of 197 rows (0 to 196, 197 to 393, ...) at most 148 rows name the same one
- priority: int32 [6304, 2], P(('group', 'expert')), may hold values from 0 to 1575, as said below
- cotangent: bfloat16 [6304, 768], P(('group', 'expert')), may hold values from -6 to 6
Outputs:
- output: bfloat16 [6304, 768], P(('group', 'expert'))
- grad_images: float32 [6304, 768], P(('group', 'expert'))
- grad_first_gain: float32 [768], P('group')
- grad_first_shift: float32 [768], P('group')
- grad_qkv: float32 [768, 2304], P('group')
- grad_proj: float32 [768, 768], P('group')
- grad_proj_bias: float32 [768], P('group')
- grad_second_gain: float32 [768], P('group')
- grad_second_shift: float32 [768], P('group')
- grad_router: float32 [768, 4], P('group')
- grad_up: float32 [4, 768, 3072], P('expert', 'group')
- grad_up_bias: float32 [4, 3072], P('expert', 'group')
- grad_down: float32 [4, 3072, 768], P('expert', 'group')
- grad_down_bias: float32 [4, 768], P('expert', 'group')
The draws below stay inside these ranges and needn't reach their ends.
Inputs may be any that keep to these rules, and one draw needn't show every extreme that they name: `expert_ids`: the two ids of a token differ. Among the rows of one device no id appears more than 148 times, and some id appears exactly 148 times. `priority`: in each aligned block of 788 tokens, the first column is a permutation of 0 to 787 and the second column a permutation of 788 to 1575.
All inputs are finite; a program needn't handle non-finite values.
Results may differ from the reference program's by a relative error of at most 0.02.
Values may be sent and summed in bfloat16 or wider, within the bound.
No kernel may reach another device: no remote copies, remote signals or barrier semaphores. Data moves between devices by JAX's collectives and lax.ppermute only.
A program may use at most 128 MiB of HBM per device.

```python
import math
import jax
import jax.numpy as jnp
import numpy as np
from jax import lax

HEADS = 12
HEAD_DIM = 64
D = 768
FF = 3072
IMG_LEN = 197
TOK_DEV = 197
TOKENS = 6304
EXPERTS = 4
GROUP_TOK = 788
CAPACITY = 394
SLOTS = 148


def draw_priority(key, part):
    block_total = TOKENS // GROUP_TOK
    key_list = jax.random.split(key, block_total * 2)
    orders = jax.vmap(lambda block_key: jax.random.permutation(block_key, GROUP_TOK))(key_list)
    orders = orders.astype(jnp.int32).reshape(block_total, 2, GROUP_TOK)
    orders = orders + (jnp.arange(2, dtype=jnp.int32) * GROUP_TOK)[None, :, None]
    return jnp.transpose(orders, (0, 2, 1)).reshape(TOKENS, 2).astype(jnp.int32)


def block_levels(own_key, extent, cuts, smallest, top_value):
    loudness, own = 1.0, jax.random.fold_in(own_key, 6)
    for axis_at, shards_of in cuts:
        heights = jnp.exp(jax.random.uniform(jax.random.fold_in(own, axis_at), (shards_of,), jnp.float32, smallest / len(cuts), top_value / len(cuts)))
        loudness = loudness * jnp.repeat(heights, extent[axis_at] // shards_of).reshape([-1 if axis == axis_at else 1 for axis in range(len(extent))])
    return loudness


def deal_out(own_key, own, number, rows, count, top, bound, slope):
    sequence = jax.random.permutation(own_key, count)
    crowded, usual = portions_of(count, rows * top, bound, slope, True), portions_of(count, rows * top, bound, slope, False)
    places = jnp.arange(count)

    def named(lengths, offset_by):
        used = int((lengths > 0).sum())
        fixed = max(1, used // 4)
        shifted = fixed + (places - fixed + offset_by * (used - fixed)) % max(1, count - fixed)
        return jnp.zeros((count,), jnp.int32).at[sequence[jnp.where(places < fixed, places, shifted)]].set(jnp.asarray(lengths, jnp.int32))

    lengths = jnp.where(number % 4 == 0, named(crowded, number // 4), named(usual, number - number // 4 - 1))
    mixed = jax.random.permutation(jax.random.fold_in(own, 3), count)
    donor, taker = mixed[0:count // 2 * 2:2], mixed[1:count // 2 * 2:2]
    slack = jnp.minimum(lengths[donor] - 1, bound - lengths[taker]) // 2
    slack = jnp.where((donor == sequence[0]) | (taker == sequence[0]) | (lengths[taker] == 0), 0, jnp.maximum(slack, 0))
    shifted = jax.random.randint(jax.random.fold_in(own, 4), (count // 2,), 0, 1 << 20) % (slack + 1)
    lengths = lengths.at[donor].add(-shifted).at[taker].add(shifted)
    members = jnp.searchsorted(jnp.cumsum(lengths), jnp.arange(rows * top), side="right").astype(jnp.int32)
    grid = members.reshape(top, rows).T
    grid = grid[jax.random.permutation(jax.random.fold_in(own, 1), rows)]
    offset_by = jax.random.randint(jax.random.fold_in(own, 2), (rows, 1), 0, top)
    return jnp.take_along_axis(grid, (jnp.arange(top)[None, :] + offset_by) % top, axis=1)


def portions_of(number_of, total, bound, slope, full):
    loads = [(1 << 20) // math.isqrt(grade ** slope) + 1 for grade in range(1, number_of + 1)]
    largest = bound if full else min(bound, max(-(-total // number_of), total * loads[0] // sum(loads)))
    least = 1 if total - largest >= number_of - 1 else 0
    given, spare = [largest] + [least] * (number_of - 1), total - largest - least * (number_of - 1)
    while spare > 0:
        candidates = [i for i in range(1, number_of) if given[i] < largest] or [i for i in range(1, number_of) if given[i] < bound]
        mass, left = sum([loads[i] for i in candidates]), spare
        for i in candidates:
            more = min(bound - given[i], max(1, left * loads[i] // mass), spare)
            given[i] = given[i] + more
            spare = spare - more
    return np.array(given)


def noise(key, dims, scale, bound, pieces=(), kind=jnp.bfloat16):
    factor_of = block_levels(key, dims, pieces, -0.22, 0.18) if pieces else 1.0
    drawn = jax.random.normal(key, dims, jnp.float32) * scale * factor_of
    return jnp.minimum(jnp.maximum(drawn, -bound), bound).astype(kind)


def setup_inputs(seed: int = 0) -> dict:
    keys = jax.random.split(jax.random.key(seed), 17)
    images = noise(keys[0], (TOKENS, D), 1.0, 6.0, ((0, 32),))
    first_gain = jnp.clip(1.0 + 0.1 * jax.random.normal(keys[1], (D,), jnp.float32), 0.5, 1.5)
    first_shift = noise(keys[2], (D,), 0.3, 1.75, (), jnp.float32)
    qkv_weight = noise(keys[3], (D, 3 * D), D ** -0.5, 0.21875)
    proj_weight = noise(keys[4], (D, D), (D // 16) ** -0.5, 0.875)
    proj_bias = noise(keys[5], (D,), 0.3, 1.75, (), jnp.float32)
    second_gain = jnp.clip(1.0 + 0.1 * jax.random.normal(keys[6], (D,), jnp.float32), 0.5, 1.5)
    second_shift = noise(keys[7], (D,), 0.3, 1.75, (), jnp.float32)
    router_weight = noise(keys[8], (D, EXPERTS), (2 * D) ** -0.5, 0.15625)
    expert_up = noise(keys[9], (EXPERTS, D, FF), D ** -0.5, 0.21875, ((0, 4),))
    up_bias = noise(keys[10], (EXPERTS, FF), 0.1, 0.625, ((0, 4),), jnp.float32)
    expert_down = noise(keys[11], (EXPERTS, FF, D), (FF // 64) ** -0.5, 0.875, ((0, 4),))
    down_bias = noise(keys[12], (EXPERTS, D), 0.3, 1.75, ((0, 4),), jnp.float32)
    expert_ids_keys = jax.random.split(jax.random.fold_in(keys[13], 1), TOKENS // TOK_DEV)
    expert_ids_turns = jax.random.permutation(jax.random.fold_in(keys[13], 3), TOKENS // TOK_DEV)
    expert_ids = jax.vmap(lambda own, number: deal_out(jax.random.fold_in(keys[13], 2), own, number, TOK_DEV, EXPERTS, 2, SLOTS, 1))(expert_ids_keys, expert_ids_turns).reshape((TOKENS, 2))
    priority = draw_priority(jax.random.fold_in(keys[16], 71), 0)
    cotangent = noise(keys[15], (TOKENS, D), 1.0, 6.0, ((0, 32),))
    return dict(images=images, first_gain=first_gain, first_shift=first_shift, qkv_weight=qkv_weight, proj_weight=proj_weight, proj_bias=proj_bias, second_gain=second_gain, second_shift=second_shift, router_weight=router_weight, expert_up=expert_up, up_bias=up_bias, expert_down=expert_down, down_bias=down_bias, expert_ids=expert_ids, priority=priority, cotangent=cotangent)


@jax.custom_vjp
def low(v):
    return lax.optimization_barrier(v.astype(jnp.bfloat16)).astype(jnp.float32)

@jax.custom_vjp
def low_back(v):
    return v

def low_keep(v):
    return (low(v), None)

def low_pass(kept, grad):
    return (grad,)

def back_keep(v):
    return (v, None)

def back_low(kept, grad):
    return (low(grad),)
low.defvjp(low_keep, low_pass)
low_back.defvjp(back_keep, back_low)
EPS = 1e-06
HIGH = lax.Precision.HIGHEST

def layer_norm(values, gain, shift):
    center = lax.optimization_barrier(jnp.mean(values, axis=-1, keepdims=True))
    centered = values - center
    spread = lax.optimization_barrier(jnp.mean(centered * centered, axis=-1, keepdims=True))
    return centered * lax.rsqrt(spread + EPS) * gain + shift

def route_ranks(group_ids, group_prio):
    pair_total = group_ids.shape[0] * 2
    flat_ids = group_ids.reshape(pair_total).astype(jnp.int32)
    flat_prio = group_prio.reshape(pair_total).astype(jnp.int32)
    inverse = jnp.zeros((pair_total,), jnp.int32).at[flat_prio].set(jnp.arange(pair_total, dtype=jnp.int32))
    sorted_ids = flat_ids[inverse]
    onehot = (sorted_ids[:, None] == jnp.arange(EXPERTS, dtype=jnp.int32)[None, :]).astype(jnp.int32)
    before = (jnp.cumsum(onehot, axis=0) - onehot).astype(jnp.int32)
    return before[flat_prio, flat_ids].reshape(group_ids.shape).astype(jnp.int32)

def group_forward(params, inputs, group_ids, group_slot, group_kept):
    first_gain, first_shift, qkv_weight, proj_weight, proj_bias, second_gain, second_shift, router_weight, expert_up, up_bias, expert_down, down_bias = params
    tok_count = inputs.shape[0]
    image_count = tok_count // IMG_LEN
    attn_in = low(layer_norm(inputs, first_gain, first_shift))
    qkv_rows = low_back(low(jnp.dot(attn_in, qkv_weight, precision=HIGH)))
    head_parts = qkv_rows.reshape(image_count, IMG_LEN, 3, HEADS, HEAD_DIM)
    scores = low_back(jnp.einsum('ilhd,imhd->ihlm', head_parts[:, :, 0], head_parts[:, :, 1], precision=HIGH) * HEAD_DIM ** (-0.5))
    attn_probs = low(jax.nn.softmax(scores, axis=-1))
    context = low_back(low(jnp.einsum('ihlm,imhd->ilhd', attn_probs, head_parts[:, :, 2], precision=HIGH).reshape(tok_count, D)))
    hidden = inputs + low_back(jnp.dot(context, proj_weight, precision=HIGH) + proj_bias)
    moe_in = low(layer_norm(hidden, second_gain, second_shift))
    router_probs = jax.nn.softmax(low_back(jnp.dot(moe_in, router_weight, precision=HIGH)), axis=-1)
    selector = (group_ids[:, :, None] == jnp.arange(EXPERTS, dtype=jnp.int32)[None, None, :]).astype(jnp.float32)
    gate_values = lax.optimization_barrier(jnp.sum(router_probs[:, None, :] * selector, axis=-1)) * group_kept
    buffers = jnp.zeros((EXPERTS, CAPACITY, D), jnp.float32)
    for column in range(2):
        buffers = buffers.at[group_ids[:, column], group_slot[:, column]].add(low_back(moe_in) * group_kept[:, column, None])
    pre_act = low_back(jnp.einsum('ecd,edf->ecf', buffers, expert_up, precision=HIGH) + up_bias[:, None, :])
    activated = low(jax.nn.gelu(pre_act, approximate=True))
    expert_res = low_back(low(jnp.einsum('ecf,efd->ecd', activated, expert_down, precision=HIGH) + down_bias[:, None, :]))
    mixture = jnp.zeros_like(hidden)
    for column in range(2):
        mixture = mixture + gate_values[:, column, None] * expert_res[group_ids[:, column], group_slot[:, column]]
    return hidden + mixture

def reference(images, first_gain, first_shift, qkv_weight, proj_weight, proj_bias, second_gain, second_shift, router_weight, expert_up, up_bias, expert_down, down_bias, expert_ids, priority, cotangent):
    group_total = TOKENS // GROUP_TOK
    ids_grouped = expert_ids.reshape(group_total, GROUP_TOK, 2).astype(jnp.int32)
    prio_grouped = priority.reshape(group_total, GROUP_TOK, 2).astype(jnp.int32)
    ranks = jax.vmap(route_ranks)(ids_grouped, prio_grouped)
    kept = (ranks < CAPACITY).astype(jnp.float32)
    slot_index = jnp.minimum(ranks, CAPACITY - 1).astype(jnp.int32)
    params = (first_gain.astype(jnp.float32), first_shift.astype(jnp.float32), qkv_weight.astype(jnp.float32), proj_weight.astype(jnp.float32), proj_bias.astype(jnp.float32), second_gain.astype(jnp.float32), second_shift.astype(jnp.float32), router_weight.astype(jnp.float32), expert_up.astype(jnp.float32), up_bias.astype(jnp.float32), expert_down.astype(jnp.float32), down_bias.astype(jnp.float32))

    def forward(weights, inputs):
        grouped = inputs.reshape(group_total, GROUP_TOK, D)

        def one_group(group_item):
            return group_forward(weights, group_item[0], group_item[1], group_item[2], group_item[3])
        results = lax.map(jax.checkpoint(one_group), (grouped, ids_grouped, slot_index, kept))
        return results.reshape(TOKENS, D)
    result, pullback = jax.vjp(forward, params, images.astype(jnp.float32))
    param_grads, input_grad = pullback(cotangent.astype(jnp.float32))
    return (result.astype(jnp.bfloat16), input_grad, param_grads[0], param_grads[1], param_grads[2], param_grads[3], param_grads[4], param_grads[5], param_grads[6], param_grads[7], param_grads[8], param_grads[9], param_grads[10], param_grads[11])
```

```python
import jax
import jax.numpy as jnp
from jax import lax
from jax.sharding import PartitionSpec as P

HEADS = 12
HEAD_DIM = 64
IMG_LEN = 197
EPS = 1e-06
BF = jnp.bfloat16
F32 = jnp.float32


def layer_norm(values, gain, shift):
    center = jnp.mean(values, axis=-1, keepdims=True)
    centered = values - center
    spread = jnp.mean(centered * centered, axis=-1, keepdims=True)
    return centered * lax.rsqrt(spread + EPS) * gain + shift


def gelu_tanh(values):
    return jax.nn.gelu(values, approximate=True)


def dot(a, b, dims):
    return lax.dot_general(a, b, (dims, ((), ())), preferred_element_type=F32)


def group_split(size):
    rows = 1
    while rows * rows * 4 <= size:
        rows *= 2
    return size // rows, rows


def expert_swap(value, mask):
    size = lax.axis_size("expert")
    return lax.ppermute(value, "expert", [(i, i ^ mask) for i in range(size)])


def expert_gather(value):
    chips = lax.axis_size("expert") // 2
    far = [value] + [expert_swap(value, 2 * k) for k in range(1, chips)]
    blocks = []
    for k in range(chips):
        blocks += [far[k], expert_swap(far[k], 1)]
    return blocks


def expert_return(blocks):
    chips = lax.axis_size("expert") // 2
    odd = jnp.stack([blocks[2 * k + 1] for k in range(chips)])
    odd = expert_swap(odd, 1)
    sums = [(blocks[2 * k].astype(F32) + odd[k].astype(F32)) for k in range(chips)]
    total = sums[0]
    for k in range(1, chips):
        total = total + expert_swap(sums[k].astype(BF), 2 * k).astype(F32)
    return total


def pick(value, index, axis):
    return lax.dynamic_index_in_dim(value, index, axis, keepdims=False)


def group_reduce(chunk):
    size = lax.axis_size("group")
    deep, wide = group_split(size)
    me = lax.axis_index("group")
    my_z, my_y = me // wide, me % wide
    mine = pick(chunk, my_y, 1)
    for k in range(1, wide):
        got = lax.ppermute(pick(chunk, my_y ^ k, 1), "group", [(i, i ^ k) for i in range(size)])
        mine = (mine.astype(F32) + got.astype(F32)).astype(BF)
    up_list = [(i, i + wide) for i in range(size - wide)]
    down_list = [(i + wide, i) for i in range(size - wide)]
    up = down = None
    for step in range(1, deep):
        part = pick(mine, jnp.minimum(my_z + deep - step, deep - 1), 0)
        if up is not None:
            part = (part.astype(F32) + up.astype(F32)).astype(BF)
        part_down = pick(mine, jnp.maximum(my_z - deep + step, 0), 0)
        if down is not None:
            part_down = (part_down.astype(F32) + down.astype(F32)).astype(BF)
        up = lax.ppermute(part, "group", up_list)
        down = lax.ppermute(part_down, "group", down_list)
    return pick(mine, my_z, 0).astype(F32) + up.astype(F32) + down.astype(F32)


def body(
    images,
    first_gain,
    first_shift,
    qkv_weight,
    proj_weight,
    proj_bias,
    second_gain,
    second_shift,
    router_weight,
    expert_up,
    up_bias,
    expert_down,
    down_bias,
    expert_ids,
    priority,
    cotangent,
):
    rows = images.shape[0]
    width = images.shape[1]
    image_count = rows // IMG_LEN
    ranks = lax.axis_size("expert")
    groups = lax.axis_size("group")
    deep, wide = group_split(groups)
    experts = router_weight.shape[1]
    hidden_width = expert_up.shape[2]
    capacity = 2 * rows
    slots = (capacity + 15) // 16 * 16
    scale = HEAD_DIM ** (-0.5)
    own = lax.axis_index("expert")

    meta = jnp.concatenate([expert_ids, priority], axis=1).T
    meta_all = jnp.concatenate(expert_gather(meta), axis=1)
    grads_all = jnp.concatenate(expert_gather(cotangent), axis=0)

    inputs = images.astype(F32)
    attn_in = layer_norm(inputs, first_gain, first_shift).astype(BF)
    qkv = dot(attn_in, qkv_weight, ((1,), (0,))).astype(BF)
    parts = qkv.reshape(image_count, IMG_LEN, 3, HEADS, HEAD_DIM)
    queries, keys, values = parts[:, :, 0], parts[:, :, 1], parts[:, :, 2]
    scores = jnp.einsum("ilhd,imhd->ihlm", queries, keys, preferred_element_type=F32) * scale
    probs = jax.nn.softmax(scores, axis=-1)
    probs_low = probs.astype(BF)
    context = jnp.einsum("ihlm,imhd->ilhd", probs_low, values, preferred_element_type=F32)
    context = context.astype(BF).reshape(rows, width)
    hidden = inputs + dot(context, proj_weight, ((1,), (0,))) + proj_bias
    moe_in = layer_norm(hidden, second_gain, second_shift).astype(BF)
    router_probs = jax.nn.softmax(dot(moe_in, router_weight, ((1,), (0,))), axis=-1)

    moe_all = jnp.concatenate(expert_gather(moe_in), axis=0)
    factor_all = jnp.concatenate(
        expert_gather(jnp.concatenate([attn_in, context], axis=1)), axis=0
    )

    first, second = meta_all[0] == own, meta_all[1] == own
    big = jnp.int32(1 << 20)
    order = jnp.where(first, meta_all[2], jnp.where(second, meta_all[3], big))
    rank = jnp.sum((order[:, None] < order[None, :]).astype(jnp.int32), axis=0)
    rank = jnp.where((order < big) & (rank < capacity), rank, -1)
    choose = (jnp.arange(slots, dtype=jnp.int32)[:, None] == rank[None, :]).astype(BF)

    taken = dot(choose, moe_all, ((1,), (0,))).astype(BF)
    taken_grad = dot(choose, grads_all, ((1,), (0,)))
    gates = jax.nn.softmax(dot(taken, router_weight, ((1,), (0,))), axis=-1)
    mine_mask = (jnp.arange(experts) == own).astype(F32)[None, :]
    gate = jnp.sum(gates * mine_mask, axis=-1, keepdims=True)
    out_grad = (gate * taken_grad).astype(BF)

    up_matrix, down_matrix = expert_up[0], expert_down[0]
    pre = dot(taken, up_matrix, ((1,), (0,))) + up_bias[0]
    act = gelu_tanh(pre).astype(BF)
    grad_down = dot(act, out_grad, ((0,), (0,))).astype(BF)
    grad_down = grad_down.reshape(deep, wide, hidden_width // groups, width)
    act_grad = dot(out_grad, down_matrix, ((1,), (1,)))
    _, gelu_back = jax.vjp(gelu_tanh, pre)
    pre_grad_full = gelu_back(act_grad)[0]
    pre_grad = pre_grad_full.astype(BF)
    grad_up = dot(taken, pre_grad, ((0,), (0,))).astype(BF)
    grad_up = grad_up.reshape(deep, wide, width // groups, hidden_width)
    up_bias_grad = jnp.sum(pre_grad.astype(F32), axis=0)
    down_bias_grad = jnp.sum(out_grad.astype(F32), axis=0)

    expert_out = (dot(act, down_matrix, ((1,), (0,))) + down_bias[0]).astype(BF)
    row_grad = dot(pre_grad, up_matrix, ((1,), (1,))).astype(BF)
    gate_grad = jnp.sum(taken_grad * expert_out.astype(F32), axis=-1, keepdims=True)
    gate_high = gate_grad.astype(BF)
    gate_low = (gate_grad - gate_high.astype(F32)).astype(BF)
    lane = jnp.arange(128)[None, :]
    extra = jnp.where(lane == own, gate_high, jnp.where(lane == own + 64, gate_low, jnp.zeros((), BF)))
    back = dot(choose, jnp.concatenate([row_grad, extra], axis=1), ((0,), (0,))).astype(BF)
    mixed = (gate * expert_out.astype(F32)).astype(BF)
    mixed = dot(choose, mixed, ((0,), (0,))).astype(BF)
    back = expert_return(jnp.split(back, ranks, axis=0))
    mixture = expert_return(jnp.split(mixed, ranks, axis=0))
    output = (hidden + mixture).astype(BF)

    pieces = 3
    down_parts = [group_reduce(c) for c in jnp.split(grad_down, pieces, axis=3)]
    up_parts = [group_reduce(c) for c in jnp.split(grad_up, pieces, axis=3)]
    grad_down_out = jnp.concatenate(down_parts, axis=1)
    grad_up_out = jnp.concatenate(up_parts, axis=1)

    moe_grad = back[:, :width]
    prob_grad = back[:, width : width + experts] + back[:, width + 64 : width + 64 + experts]
    upstream = cotangent.astype(F32)
    logit_grad = router_probs * (
        prob_grad - jnp.sum(router_probs * prob_grad, axis=-1, keepdims=True)
    )
    logit_grad = logit_grad.astype(BF)
    grad_router = dot(moe_in, logit_grad, ((0,), (0,)))
    norm_two_grad = dot(logit_grad, router_weight, ((1,), (1,))) + moe_grad
    _, norm_two_back = jax.vjp(layer_norm, hidden, second_gain, second_shift)
    hidden_grad, grad_second_gain, grad_second_shift = norm_two_back(norm_two_grad)
    hidden_grad = hidden_grad + upstream
    proj_grad = hidden_grad.astype(BF)
    grad_proj_bias = jnp.sum(proj_grad.astype(F32), axis=0)
    context_grad = dot(proj_grad, proj_weight, ((1,), (1,))).astype(BF)
    context_grad = context_grad.reshape(image_count, IMG_LEN, HEADS, HEAD_DIM)
    value_grad = jnp.einsum("ihlm,ilhd->imhd", probs_low, context_grad, preferred_element_type=F32)
    prob_back = jnp.einsum("ilhd,imhd->ihlm", context_grad, values, preferred_element_type=F32)
    score_grad = probs * (prob_back - jnp.sum(probs * prob_back, axis=-1, keepdims=True))
    score_grad = score_grad.astype(BF)
    query_grad = jnp.einsum("ihlm,imhd->ilhd", score_grad, keys, preferred_element_type=F32) * scale
    key_grad = jnp.einsum("ihlm,ilhd->imhd", score_grad, queries, preferred_element_type=F32) * scale
    qkv_grad = jnp.stack([query_grad, key_grad, value_grad], axis=2).astype(BF)
    qkv_grad = qkv_grad.reshape(rows, 3 * width)
    norm_one_grad = dot(qkv_grad, qkv_weight, ((1,), (1,)))
    _, norm_one_back = jax.vjp(layer_norm, inputs, first_gain, first_shift)
    input_grad, grad_first_gain, grad_first_shift = norm_one_back(norm_one_grad)
    grad_images = input_grad + hidden_grad

    def share(value):
        columns = value.shape[1] // ranks
        split = jnp.transpose(value.reshape(rows, ranks, columns), (1, 0, 2))
        got = [pick(split, own, 0)]
        for j in range(1, ranks):
            got.append(expert_swap(pick(split, own ^ j, 0), j))
        return jnp.concatenate(got, axis=0)

    proj_share = share(proj_grad)
    qkv_share = share(qkv_grad)
    small = jnp.stack(
        [grad_first_gain, grad_first_shift, grad_proj_bias, grad_second_gain, grad_second_shift]
        + [grad_router[:, i] for i in range(experts)]
    )
    small_all = expert_gather(small)
    small_sum = small_all[0]
    for other in small_all[1:]:
        small_sum = small_sum + other
    up_cols = up_bias_grad.reshape(groups, hidden_width // width, width // groups)
    up_cols = jnp.transpose(up_cols, (1, 0, 2)).reshape(hidden_width // width, width)
    small_rows = jnp.concatenate([small_sum, up_cols, down_bias_grad[None]], axis=0)
    count = small_rows.shape[0]
    qkv_part = dot(factor_all[:, :width], qkv_share, ((0,), (0,))).astype(BF)
    proj_part = dot(factor_all[:, width:], proj_share, ((0,), (0,))).astype(BF)
    small_cols = jnp.pad(small_rows.T, ((0, 0), (0, 128 - count))).astype(BF)
    shared = jnp.concatenate([qkv_part, proj_part, small_cols], axis=1)
    columns = shared.shape[1]
    total = group_reduce(shared.reshape(deep, wide, width // groups, columns))
    small_total = total[:, columns - 128 :]
    qkv_columns = 3 * width // ranks
    blocks = expert_gather(total[:, : columns - 128].astype(BF))
    stacked = jnp.stack(blocks)
    order_of = own ^ jnp.arange(ranks)
    ordered = jnp.stack([pick(stacked, order_of[b], 0) for b in range(ranks)])
    grad_qkv = jnp.concatenate([ordered[b][:, :qkv_columns] for b in range(ranks)], axis=1).astype(F32)
    grad_proj = jnp.concatenate([ordered[b][:, qkv_columns:] for b in range(ranks)], axis=1).astype(F32)
    at = 5 + experts
    grad_up_bias = small_total[:, at : at + hidden_width // width].T.reshape(1, -1)
    grad_down_bias = small_total[:, at + hidden_width // width][None]
    return (
        output,
        grad_images,
        small_total[:, 0],
        small_total[:, 1],
        grad_qkv,
        grad_proj,
        small_total[:, 2],
        small_total[:, 3],
        small_total[:, 4],
        small_total[:, 5 : 5 + experts],
        grad_up_out[None],
        grad_up_bias,
        grad_down_out[None],
        grad_down_bias,
    )


def solution(mesh):
    in_specs = (
        P(("group", "expert"), None),
        P(),
        P(),
        P(),
        P(),
        P(),
        P(),
        P(),
        P(),
        P("expert", None, None),
        P("expert", None),
        P("expert", None, None),
        P("expert", None),
        P(("group", "expert"), None),
        P(("group", "expert"), None),
        P(("group", "expert"), None),
    )
    out_specs = (
        P(("group", "expert"), None),
        P(("group", "expert"), None),
        P("group"),
        P("group"),
        P("group", None),
        P("group", None),
        P("group"),
        P("group"),
        P("group"),
        P("group", None),
        P("expert", "group", None),
        P("expert", "group"),
        P("expert", "group", None),
        P("expert", "group"),
    )
    return jax.shard_map(body, mesh=mesh, in_specs=in_specs, out_specs=out_specs, check_vma=False)
```
